128 devices in a mesh: row: 8 (over z, core), col: 16 (over x, y).
Axes of the slice: x: 4, y: 4, z: 4, core: 2. Of those that a mesh axis runs over, the one named last changes fastest.
Arguments:
- factor_strip: float32 [4, 3, 512, 4096], P(None, None, 'col', 'row'), may hold values from -0.4375 to 0.4375
- pivots: float32 [3, 512], replicated, may hold values from 1 to 4
- right_side: float32 [4, 4096, 16384], P(None, 'row', 'col'), may hold values from -6 to 6
Outputs:
- solved: float32 [3, 512, 16384], P(None, None, 'col')
- trailing: float32 [4, 4096, 16384], P(None, 'row', 'col')
The draws below stay inside these ranges and needn't reach their ends.
All inputs are finite; a program needn't handle non-finite values.
Results may differ from the reference program's by a relative error of at most 0.0001.
Values sent between devices are 32-bit elements; how exact they have to be, the bound alone decides.
No kernel may reach another device: no remote copies, remote signals or barrier semaphores. Data moves between devices by JAX's collectives and lax.ppermute only.
A program may use at most 128 MiB of HBM per device.

```python
import math
import jax
import jax.numpy as jnp
from jax import lax

PANEL = 512
PANELS = 3
RB_DEV = 4
M_ROW = 4096
NC = 16384
N_ROW = 8


def steps_of(stream_key, extent, shards, smallest, top_value):
    gain = 1.0
    for position, blocks in shards:
        heights = jax.random.uniform(jax.random.fold_in(jax.random.fold_in(stream_key, 6), position), (blocks,), jnp.float32, smallest / len(shards), top_value / len(shards))
        gain = gain * jnp.repeat(jnp.exp(heights), extent[position] // blocks).reshape((-1,) + (1,) * (len(extent) - 1 - position))
    return gain


def centred(own_key, shape, width, limit, split=(), kind=jnp.bfloat16):
    gain = steps_of(own_key, shape, split, -0.22, 0.18) if split else 1.0
    array = jax.random.normal(own_key, shape, jnp.float32) * width * gain
    return jnp.minimum(jnp.maximum(array, -limit), limit).astype(kind)


def setup_inputs(seed: int = 0) -> dict:
    key_of = jax.random.split(jax.random.key(seed), 4)
    return {
        "factor_strip": centred(key_of[0], (RB_DEV, PANELS, PANEL, M_ROW), 0.03, 0.4375, ((2, 16), (3, 8)), jnp.float32),
        "pivots": jnp.clip(jnp.exp(jax.random.uniform(key_of[1], (PANELS, PANEL), jnp.float32, math.log(1.0), math.log(4.0))), 1.0, 4.0),
        "right_side": centred(key_of[2], (RB_DEV, M_ROW, NC), 1.0, 6.0, ((1, 8), (2, 16)), jnp.float32),
    }


def reference(factor_strip, pivots, right_side):
    blocks = jnp.arange(RB_DEV, dtype=jnp.int32)[:, None] * N_ROW + (jnp.arange(M_ROW, dtype=jnp.int32) // PANEL)[None, :]
    work = right_side
    outputs = []
    for panel_index in range(PANELS):
        panel = factor_strip[:, panel_index]
        square = panel[0, :, panel_index * PANEL:(panel_index + 1) * PANEL].T
        lower = jnp.tril(square, -1) + jnp.diag(pivots[panel_index])
        target = work[0, panel_index * PANEL:(panel_index + 1) * PANEL]
        result = jax.scipy.linalg.solve_triangular(lower, target, lower=True)
        outputs.append(result)
        update = jnp.einsum('bcr,cn->brn', panel, result, precision=lax.Precision.HIGHEST)
        keep = (blocks > panel_index)[:, :, None]
        work = jnp.where(keep, work - update, work)
    return (jnp.stack(outputs), work)
```

```python
import functools

import jax
import jax.numpy as jnp
from jax import lax
from jax.experimental import pallas as pl
from jax.experimental.pallas import tpu as pltpu
from jax.sharding import PartitionSpec as P


F32, BF16 = jnp.float32, jnp.bfloat16
PANELS, PANEL, SHARE, HALF, NCOL = 3, 512, 32, 512, 1024
AXES = ("row", "col")
TN = (((0,), (0,)), ((), ()))
NN = (((1,), (0,)), ((), ()))

X1, X3, Y1, Y3 = 4, 12, 1, 3
STEPS = {
    (0, 0): (X1, X3, Y1, Y3),
    (0, 1): (Y1, Y3, X1, X3),
    (1, 0): (X3, X1, Y3, Y1),
    (1, 1): (Y3, Y1, X3, X1),
}
OFFSETS = (0, 3, 1, 2)


def permute(value, target):
    pairs = []
    for row in range(8):
        for col in range(16):
            r, c = target(row, col)
            pairs.append((row * 16 + col, r * 16 + c))
    return lax.ppermute(value, AXES, pairs)


def xor_wave(value, color, k):
    return permute(value, lambda r, c: (r, c ^ STEPS[(r % 2, color)][k]))


def swap_cores(value):
    return permute(value, lambda r, c: (r ^ 1, c))


def z_xor(value, mask):
    return permute(value, lambda r, c: (r ^ (2 * mask), c))


def z_ring(value):
    def target(r, c):
        z, core = r // 2, r % 2
        return ((z + (1 if core == 0 else 3)) % 4) * 2 + core, c

    return permute(value, target)


def shift(value, phase, s):
    def target(r, c):
        x, y = c // 4, c % 4
        if (r % 2 + phase) % 2 == 0:
            x = (x + s) % 4
        else:
            y = (y + s) % 4
        return r, x * 4 + y

    return permute(value, target)


def split(v):
    hi = v.astype(BF16)
    return hi, (v - hi.astype(F32)).astype(BF16)


def dot3(a, b, dims):
    ah, al = a
    bh, bl = b
    out = lax.dot_general(ah, bh, dims, preferred_element_type=F32)
    out += lax.dot_general(ah, bl, dims, preferred_element_type=F32)
    out += lax.dot_general(al, bh, dims, preferred_element_type=F32)
    return out


BLOCK = {(0, 0): 0, (0, 2): 1, (1, 2): 2, (0, 1): 3, (1, 1): 4, (2, 2): 5}


def join_body(groups, *refs):
    count = sum(len(g) for g in groups)
    ins, outs, sem = refs[:count], refs[count:-1], refs[-1]
    copies, k = [], 0
    for g, out in zip(groups, outs):
        at = 0
        for n in g:
            copies.append(pltpu.make_async_copy(ins[k], out.at[pl.ds(at, n)], sem))
            at += n
            k += 1
    for c in copies:
        c.start()
    for c in copies:
        c.wait()


def join(*groups):
    flat = [v for g in groups for v in g]
    sizes = tuple(tuple(v.shape[0] for v in g) for g in groups)
    outs = [jax.ShapeDtypeStruct((sum(n),) + g[0].shape[1:], F32) for n, g in zip(sizes, groups)]
    size = sum(v.size for v in flat) * 4
    return pl.pallas_call(
        functools.partial(join_body, sizes),
        out_shape=outs,
        in_specs=[pl.BlockSpec(memory_space=pl.ANY)] * len(flat),
        out_specs=[pl.BlockSpec(memory_space=pltpu.VMEM)] * len(outs),
        scratch_shapes=[pltpu.SemaphoreType.DMA],
        compiler_params=pltpu.CompilerParams(vmem_limit_bytes=size + (1 << 20)),
        cost_estimate=pl.CostEstimate(flops=0, bytes_accessed=2 * size, transcendentals=0),
    )(*flat)


def pack_body(tab, *refs):
    ins, out, sem = refs[:4], refs[4], refs[5]
    copies = []
    for k in range(4):
        for j in range(4):
            src = pl.ds(pl.multiple_of(tab[4 + 4 * k + j] * SHARE, SHARE), SHARE)
            copies.append(pltpu.make_async_copy(ins[k].at[j], out.at[:, src, :], sem))
    for c in copies:
        c.start()
    for c in copies:
        c.wait()


def pack(tab, parts):
    size = PANELS * PANEL * PANEL * 4
    return pl.pallas_call(
        pack_body,
        out_shape=jax.ShapeDtypeStruct((PANELS, PANEL, PANEL), F32),
        in_specs=[pl.BlockSpec(memory_space=pltpu.SMEM)] + [pl.BlockSpec(memory_space=pl.ANY)] * 4,
        out_specs=pl.BlockSpec(memory_space=pltpu.VMEM),
        scratch_shapes=[pltpu.SemaphoreType.DMA],
        compiler_params=pltpu.CompilerParams(vmem_limit_bytes=size + (1 << 20)),
        cost_estimate=pl.CostEstimate(flops=0, bytes_accessed=2 * size, transcendentals=0),
        name="pack",
    )(tab, *parts)


def prep_body(tab, piv, own, other, lh_o, ll_o, vh_o, vl_o, lv, lh, ll, vh, vl, sem):
    core = tab[0]
    ca = pltpu.make_async_copy(own, lv.at[pl.ds(3 * core, 3)], sem.at[0])
    cb = pltpu.make_async_copy(other, lv.at[pl.ds(3 - 3 * core, 3)], sem.at[1])
    ca.start()
    cb.start()
    ca.wait()
    cb.wait()
    for n in range(6):
        hi, lo = split(lv[n])
        lh[n] = hi
        ll[n] = lo
    outs = [pltpu.make_async_copy(a, b, sem.at[2 + k])
            for k, (a, b) in enumerate(((lh, lh_o), (ll, ll_o), (vh, vh_o), (vl, vl_o)))]
    outs[0].start()
    outs[1].start()

    row32 = lax.broadcasted_iota(jnp.int32, (32, 128), 0)
    lane = lax.broadcasted_iota(jnp.int32, (32, 128), 1)
    group = lane // 32
    eye = jnp.where(lane % 32 == row32, 1.0, 0.0).astype(F32)
    r128 = lax.broadcasted_iota(jnp.int32, (128, 128), 0)
    c128 = lax.broadcasted_iota(jnp.int32, (128, 128), 1)
    blocks = [(p, d) for p in range(PANELS) for d in range(4)]
    comp, ts, pvs, vs = [], [], [], []
    for p, d in blocks:
        u = lv[BLOCK[(p, p)], 128 * d:128 * d + 128, 128 * d:128 * d + 128]
        c = jnp.zeros((32, 128), F32)
        for b in range(4):
            c = jnp.where(group == b, u[32 * b:32 * b + 32, :], c)
        comp.append(c)
        ts.append(eye)
        pvs.append(1.0 / jnp.broadcast_to(piv[p:p + 1, 128 * d:128 * d + 128], (8, 128)))
        vs.append(jnp.zeros((32, 128), F32))
    for j in range(31, -1, -1):
        idx = group * 32 + j
        for n in range(len(blocks)):
            pj = jnp.take_along_axis(pvs[n], idx[:8], axis=1)
            vj = jnp.broadcast_to(ts[n][j:j + 1, :] * pj[0:1, :], (32, 128))
            vs[n] = jnp.where(row32 == j, vj, vs[n])
            if j:
                uj = jnp.take_along_axis(comp[n], idx, axis=1)
                ts[n] = jnp.where(row32 < j, ts[n] - uj * vj, ts[n])
    full = [jnp.concatenate([jnp.where(group == b, v, 0.0) for b in range(4)], 0) for v in vs]
    for s in (32, 64):
        off = (r128 // (2 * s) == c128 // (2 * s)) & (r128 // s % 2 == 0) & (c128 // s % 2 == 1)
        ms = []
        for n, (p, d) in enumerate(blocks):
            u = lv[BLOCK[(p, p)], 128 * d:128 * d + 128, 128 * d:128 * d + 128]
            ms.append(dot3(split(jnp.where(off, u, 0.0)), split(full[n]), NN))
        full = [v - dot3(split(v), split(m), NN) for v, m in zip(full, ms)]
    for n, (p, d) in enumerate(blocks):
        hi, lo = split(full[n])
        vh[p, d] = hi
        vl[p, d] = lo
    outs[2].start()
    outs[3].start()
    for c in outs:
        c.wait()


def prep(tab, pivots, own, other):
    hbm = pl.BlockSpec(memory_space=pl.ANY)
    vmem = pl.BlockSpec(memory_space=pltpu.VMEM)
    big = jax.ShapeDtypeStruct((6, PANEL, PANEL), BF16)
    small = jax.ShapeDtypeStruct((PANELS, 4, 128, 128), BF16)
    return pl.pallas_call(
        prep_body,
        out_shape=[big, big, small, small],
        in_specs=[pl.BlockSpec(memory_space=pltpu.SMEM), vmem, hbm, hbm],
        out_specs=[pl.BlockSpec(memory_space=pltpu.HBM)] * 4,
        scratch_shapes=[
            pltpu.VMEM((6, PANEL, PANEL), F32),
            pltpu.VMEM((6, PANEL, PANEL), BF16),
            pltpu.VMEM((6, PANEL, PANEL), BF16),
            pltpu.VMEM((PANELS, 4, 128, 128), BF16),
            pltpu.VMEM((PANELS, 4, 128, 128), BF16),
            pltpu.SemaphoreType.DMA((6,)),
        ],
        compiler_params=pltpu.CompilerParams(vmem_limit_bytes=56 << 20),
        cost_estimate=pl.CostEstimate(flops=4 << 30, bytes_accessed=14 << 20, transcendentals=0),
        name="prep",
    )(tab, pivots, own, other)


def solve_body(tab, lh_h, ll_h, vh_h, vl_h, rhs, swp, r1, r2, r3, r4, out,
               lh, ll, vh, vl, rv, xh, xl, sem_l, sem_v, sem_r):
    core = tab[0]
    cands = [rhs.at[0, :, pl.ds(pl.multiple_of(core * HALF, HALF), HALF)], swp, r1, r2, r3, r4]
    vcopies = [pltpu.make_async_copy(vh_h, vh, sem_v), pltpu.make_async_copy(vl_h, vl, sem_v)]
    lcopies = {}
    for q in range(PANELS):
        for p in range(q + 1):
            n = BLOCK[(p, q)]
            lcopies[(p, q)] = [pltpu.make_async_copy(lh_h.at[n], lh.at[n], sem_l.at[n]),
                               pltpu.make_async_copy(ll_h.at[n], ll.at[n], sem_l.at[n])]
    for q in range(PANELS):
        for k, cand in enumerate(cands):
            @pl.when(tab[1 + q] == k)
            def _():
                pltpu.make_async_copy(cand.at[pl.ds(0, PANEL)], rv.at[q], sem_r.at[q]).start()
        if q == 0:
            for c in vcopies:
                c.start()
        for p in range(q + 1):
            for c in lcopies[(p, q)]:
                c.start()
    for c in vcopies:
        c.wait()
    for q in range(PANELS):
        pltpu.make_async_copy(r1.at[pl.ds(0, PANEL)], rv.at[q], sem_r.at[q]).wait()
        for p in range(q + 1):
            for c in lcopies[(p, q)]:
                c.wait()
        diag = BLOCK[(q, q)]
        for h in range(2):
            cols = slice(256 * h, 256 * h + 256)
            acc = rv[q, :, cols]
            for p in range(q):
                n = BLOCK[(p, q)]
                acc = acc - dot3((lh[n], ll[n]), (xh[p, :, cols], xl[p, :, cols]), TN)
            rv[q, :, cols] = acc
        for i in range(4):
            rows = slice(128 * i, 128 * i + 128)
            for h in range(2):
                cols = slice(256 * h, 256 * h + 256)
                t = rv[q, rows, cols]
                if i:
                    t = t - dot3((lh[diag, 0:128 * i, rows], ll[diag, 0:128 * i, rows]),
                                 (xh[q, 0:128 * i, cols], xl[q, 0:128 * i, cols]), TN)
                x = dot3((vh[q, i], vl[q, i]), split(t), TN)
                hi, lo = split(x)
                xh[q, rows, cols] = hi
                xl[q, rows, cols] = lo
                out[q, rows, cols] = x


def solve(tab, factors, rhs, swp, recvs):
    hbm = pl.BlockSpec(memory_space=pltpu.HBM)
    vmem = pl.BlockSpec(memory_space=pltpu.VMEM)
    return pl.pallas_call(
        solve_body,
        out_shape=jax.ShapeDtypeStruct((PANELS, PANEL, HALF), F32),
        in_specs=[pl.BlockSpec(memory_space=pltpu.SMEM)] + [hbm] * 10,
        out_specs=vmem,
        scratch_shapes=[
            pltpu.VMEM((6, PANEL, PANEL), BF16),
            pltpu.VMEM((6, PANEL, PANEL), BF16),
            pltpu.VMEM((PANELS, 4, 128, 128), BF16),
            pltpu.VMEM((PANELS, 4, 128, 128), BF16),
            pltpu.VMEM((PANELS, PANEL, HALF), F32),
            pltpu.VMEM((PANELS, PANEL, HALF), BF16),
            pltpu.VMEM((PANELS, PANEL, HALF), BF16),
            pltpu.SemaphoreType.DMA((6,)),
            pltpu.SemaphoreType.DMA,
            pltpu.SemaphoreType.DMA((PANELS,)),
        ],
        compiler_params=pltpu.CompilerParams(vmem_limit_bytes=56 << 20),
        cost_estimate=pl.CostEstimate(flops=8 << 30, bytes_accessed=14 << 20, transcendentals=0),
        name="solve",
    )(tab, *factors, rhs, swp, *recvs)


def update_body(tab_ref, xa_hbm, xb_hbm, *refs):
    bufs = (refs[:4], refs[4:8])
    work_ref, out_ref, solved, xv, xh, xl, fv, sem_x, sem_f = refs[8:]
    step = pl.program_id(0)
    b = step // 2
    core = tab_ref[0]
    row = tab_ref[1]
    xc = [pltpu.make_async_copy(src, xv.at[:, :, pl.ds(pl.multiple_of(h * HALF, HALF), HALF)], sem_x.at[k])
          for k, (src, h) in enumerate(((xa_hbm, core), (xb_hbm, 1 - core)))]
    out_copy = pltpu.make_async_copy(xv, solved, sem_x.at[2])

    def fcopies(color, inner, slot):
        for q in range(4):
            for i in range(4):
                s = pl.ds(pl.multiple_of(tab_ref[2 + color * 16 + q * 4 + i] * SHARE, SHARE), SHARE)
                yield pltpu.make_async_copy(bufs[color][q].at[i, inner], fv.at[slot, :, s, :], sem_f.at[slot])

    def start(which, slot):
        for color in range(2):
            for inner in range(2):
                @pl.when(which == color * 2 + inner)
                def _():
                    for c in fcopies(color, inner, slot):
                        c.start()

    slot = lax.rem(b, 2)

    @pl.when(step == 0)
    def _():
        for c in xc:
            c.start()
        start(0, 0)
        start(1, 1)
        for c in xc:
            c.wait()
        out_copy.start()
        for p in range(PANELS):
            hi, lo = split(xv[p])
            xh[p * PANEL:p * PANEL + PANEL, :] = hi
            xl[p * PANEL:p * PANEL + PANEL, :] = lo

    @pl.when(lax.rem(step, 2) == 0)
    def _():
        for c in fcopies(0, 0, slot):
            c.wait()

    cols = pl.ds(pl.multiple_of(lax.rem(step, 2) * 256, 256), 256)
    fs = []
    for p in range(PANELS):
        keep = jnp.logical_or(b > 0, row > p)
        fs.append(jnp.where(keep, fv[slot, p, :, cols], 0.0))
    up = dot3(split(jnp.concatenate(fs, 0)), (xh[...], xl[...]), TN)
    out_ref[0] = work_ref[0] - up

    @pl.when((lax.rem(step, 2) == 1) & (b + 2 < 4))
    def _():
        start(b + 2, slot)

    @pl.when(step == 7)
    def _():
        out_copy.wait()


def update(tab, xa, xb, bufs_a, bufs_b, work):
    wspec = pl.BlockSpec((1, 256, NCOL), lambda s, t: (s // 2, s % 2, 0))
    hbm = pl.BlockSpec(memory_space=pltpu.HBM)
    return pl.pallas_call(
        update_body,
        out_shape=[jax.ShapeDtypeStruct(work.shape, F32), jax.ShapeDtypeStruct((PANELS, PANEL, NCOL), F32)],
        grid_spec=pltpu.PrefetchScalarGridSpec(
            num_scalar_prefetch=1, grid=(8,),
            in_specs=[hbm] * 10 + [wspec],
            out_specs=[wspec, pl.BlockSpec(memory_space=pltpu.HBM)],
            scratch_shapes=[
                pltpu.VMEM((PANELS, PANEL, NCOL), F32),
                pltpu.VMEM((PANELS * PANEL, NCOL), BF16),
                pltpu.VMEM((PANELS * PANEL, NCOL), BF16),
                pltpu.VMEM((2, PANELS, PANEL, PANEL), F32),
                pltpu.SemaphoreType.DMA((3,)),
                pltpu.SemaphoreType.DMA((2,)),
            ],
        ),
        compiler_params=pltpu.CompilerParams(vmem_limit_bytes=60 << 20),
        cost_estimate=pl.CostEstimate(flops=20 << 30, bytes_accessed=42 << 20, transcendentals=0),
        name="update",
    )(tab, xa, xb, *bufs_a, *bufs_b, work)


def table(core, make):
    a = jnp.array(make(0), jnp.int32)
    b = jnp.array(make(1), jnp.int32)
    return jnp.where(core == 0, a, b)


def wave_masks(core, color):
    m = STEPS[(core, color)]
    low = [(m[0] if i & 1 else 0) ^ (m[1] if i & 2 else 0) for i in range(4)]
    return low, [v ^ m[2] for v in low], [v ^ m[3] for v in low], [v ^ m[2] ^ m[3] for v in low]


def panels(factor, pivots, rhs):
    row = lax.axis_index("row")
    col = lax.axis_index("col")
    core, z = row % 2, row // 2
    x, y = col // 4, col % 4
    first = core == 0

    swl = swap_cores(factor[0, 2])
    half_a, half_b = factor[0:2][None], factor[2:4][None]
    ra1 = xor_wave(half_a, 0, 0)
    pay = factor[0, 0:2]
    pay = jnp.where((core == 1) & (z == 1), jnp.broadcast_to(swl[None], pay.shape), pay)
    got = z_xor(pay, 1)
    low = jnp.where(z == 0, pay, got)
    high = jnp.where(z == 0, got, pay)
    share = jnp.where(first, jnp.stack([low[0], high[0], high[1]]), jnp.stack([low[0], low[1], high[0]]))

    slab = rhs[0]
    theirs = jnp.where(first, slab[:, HALF:], slab[:, :HALF])
    mine = jnp.where(first, slab[:, :HALF], slab[:, HALF:])
    swp = swap_cores(theirs)
    rb1 = xor_wave(half_b, 1, 0)
    share = jnp.where(z < 2, share, z_xor(share, 3))

    r1 = z_ring(jnp.where(first, mine, swp))
    r2 = z_ring(jnp.where(z == 0, jnp.where(first, swp, mine), r1))
    r3 = z_ring(jnp.where((z == 0) & (core == 1), r1, r2))
    r4 = z_ring(r3)

    def place(which):
        cols = []
        for k in range(4):
            for j in range(4):
                if which == 0:
                    cols.append((x + OFFSETS[j]) % 4 * 4 + (y + OFFSETS[k]) % 4)
                else:
                    cols.append((x + OFFSETS[k]) % 4 * 4 + (y + OFFSETS[j]) % 4)
        return jnp.stack(cols)

    rtab = jnp.array([[[0, 1, 4], [2, 3, 0], [3, 4, 2], [4, 5, 3]],
                      [[1, 0, 2], [4, 5, 1], [3, 4, 5], [2, 3, 4]]], jnp.int32)
    stab = jnp.concatenate([core[None], rtab[core, z], jnp.where(first, place(0), place(1))]).astype(jnp.int32)

    one = share[None]
    (ph1,) = join([one] + [shift(one, 0, s) for s in (1, 3, 2)])
    lown = pack(stab, [ph1] + [shift(ph1, 1, s) for s in (1, 3, 2)])
    loth = swap_cores(lown)

    fa, fb = join([half_a, ra1], [half_b, rb1])
    ra2, rb2 = xor_wave(fa, 0, 1), xor_wave(fb, 1, 1)
    fa, fb = join([fa, ra2], [fb, rb2])
    ga, gb = xor_wave(fa, 0, 2), xor_wave(fb, 1, 2)
    ha, hb = xor_wave(fa, 0, 3), xor_wave(fb, 1, 3)
    ka, kb = xor_wave(ga, 0, 3), xor_wave(gb, 1, 3)

    factors = prep(stab, pivots, lown, loth)
    xa = solve(stab, factors, rhs, swp, (r1, r2, r3, r4))
    xb = swap_cores(xa)

    def make(c):
        return [v for color in range(2) for part in wave_masks(c, color) for v in part]

    utab = jnp.concatenate([core[None], row[None], table(core, make) ^ col]).astype(jnp.int32)
    work, solved = update(utab, xa, xb, (fa, ga, ha, ka), (fb, gb, hb, kb), rhs)
    return solved, work


def solution(mesh):
    return jax.shard_map(
        panels,
        mesh=mesh,
        in_specs=(P(None, None, "col", "row"), P(), P(None, "row", "col")),
        out_specs=(P(None, None, "col"), P(None, "row", "col")),
        check_vma=False,
    )
```

```python
import functools

import jax
import jax.numpy as jnp
from jax import lax
from jax.experimental import pallas as pl
from jax.experimental.pallas import tpu as pltpu
from jax.sharding import PartitionSpec as P


F32, BF16 = jnp.float32, jnp.bfloat16
PANELS, PANEL, SHARE, HALF, NCOL = 3, 512, 32, 512, 1024
AXES = ("row", "col")
TN = (((0,), (0,)), ((), ()))
NN = (((1,), (0,)), ((), ()))

X1, X3, Y1, Y3 = 4, 12, 1, 3
STEPS = {
    (0, 0): (X1, X3, Y1, Y3),
    (0, 1): (Y1, Y3, X1, X3),
    (1, 0): (X3, X1, Y3, Y1),
    (1, 1): (Y3, Y1, X3, X1),
}
OFFSETS = (0, 3, 1, 2)


def permute(value, target):
    pairs = []
    for row in range(8):
        for col in range(16):
            r, c = target(row, col)
            pairs.append((row * 16 + col, r * 16 + c))
    return lax.ppermute(value, AXES, pairs)


def xor_wave(value, color, k):
    return permute(value, lambda r, c: (r, c ^ STEPS[(r % 2, color)][k]))


def swap_cores(value):
    return permute(value, lambda r, c: (r ^ 1, c))


def z_xor(value, mask):
    return permute(value, lambda r, c: (r ^ (2 * mask), c))


def z_ring(value):
    def target(r, c):
        z, core = r // 2, r % 2
        return ((z + (1 if core == 0 else 3)) % 4) * 2 + core, c

    return permute(value, target)


def shift(value, phase, s):
    def target(r, c):
        x, y = c // 4, c % 4
        if (r % 2 + phase) % 2 == 0:
            x = (x + s) % 4
        else:
            y = (y + s) % 4
        return r, x * 4 + y

    return permute(value, target)


def split(v):
    hi = v.astype(BF16)
    return hi, (v - hi.astype(F32)).astype(BF16)


def dot3(a, b, dims):
    ah, al = a
    bh, bl = b
    out = lax.dot_general(ah, bh, dims, preferred_element_type=F32)
    out += lax.dot_general(ah, bl, dims, preferred_element_type=F32)
    out += lax.dot_general(al, bh, dims, preferred_element_type=F32)
    return out


BLOCK = {(0, 0): 0, (0, 2): 1, (1, 2): 2, (0, 1): 3, (1, 1): 4, (2, 2): 5}


def join_body(groups, *refs):
    count = sum(len(g) for g in groups)
    ins, outs, sem = refs[:count], refs[count:-1], refs[-1]
    copies, k = [], 0
    for g, out in zip(groups, outs):
        at = 0
        for n in g:
            copies.append(pltpu.make_async_copy(ins[k], out.at[pl.ds(at, n)], sem))
            at += n
            k += 1
    for c in copies:
        c.start()
    for c in copies:
        c.wait()


def join(*groups):
    flat = [v for g in groups for v in g]
    sizes = tuple(tuple(v.shape[0] for v in g) for g in groups)
    outs = [jax.ShapeDtypeStruct((sum(n),) + g[0].shape[1:], F32) for n, g in zip(sizes, groups)]
    size = sum(v.size for v in flat) * 4
    return pl.pallas_call(
        functools.partial(join_body, sizes),
        out_shape=outs,
        in_specs=[pl.BlockSpec(memory_space=pl.ANY)] * len(flat),
        out_specs=[pl.BlockSpec(memory_space=pltpu.VMEM)] * len(outs),
        scratch_shapes=[pltpu.SemaphoreType.DMA],
        compiler_params=pltpu.CompilerParams(vmem_limit_bytes=size + (1 << 20)),
        cost_estimate=pl.CostEstimate(flops=0, bytes_accessed=2 * size, transcendentals=0),
    )(*flat)


def pack_body(tab, *refs):
    ins, out, sem = refs[:4], refs[4], refs[5]
    copies = []
    for k in range(4):
        for j in range(4):
            src = pl.ds(pl.multiple_of(tab[4 + 4 * k + j] * SHARE, SHARE), SHARE)
            copies.append(pltpu.make_async_copy(ins[k].at[j], out.at[:, src, :], sem))
    for c in copies:
        c.start()
    for c in copies:
        c.wait()


def pack(tab, parts):
    size = PANELS * PANEL * PANEL * 4
    return pl.pallas_call(
        pack_body,
        out_shape=jax.ShapeDtypeStruct((PANELS, PANEL, PANEL), F32),
        in_specs=[pl.BlockSpec(memory_space=pltpu.SMEM)] + [pl.BlockSpec(memory_space=pl.ANY)] * 4,
        out_specs=pl.BlockSpec(memory_space=pltpu.VMEM),
        scratch_shapes=[pltpu.SemaphoreType.DMA],
        compiler_params=pltpu.CompilerParams(vmem_limit_bytes=size + (1 << 20)),
        cost_estimate=pl.CostEstimate(flops=0, bytes_accessed=2 * size, transcendentals=0),
        name="pack",
    )(tab, *parts)


def prep_body(tab, piv, own, other, lh_o, ll_o, vh_o, vl_o, lv, lh, ll, vh, vl, sem):
    core = tab[0]
    ca = pltpu.make_async_copy(own, lv.at[pl.ds(3 * core, 3)], sem.at[0])
    cb = pltpu.make_async_copy(other, lv.at[pl.ds(3 - 3 * core, 3)], sem.at[1])
    ca.start()
    cb.start()
    ca.wait()
    cb.wait()
    for n in range(6):
        hi, lo = split(lv[n])
        lh[n] = hi
        ll[n] = lo
    outs = [pltpu.make_async_copy(a, b, sem.at[2 + k])
            for k, (a, b) in enumerate(((lh, lh_o), (ll, ll_o), (vh, vh_o), (vl, vl_o)))]
    outs[0].start()
    outs[1].start()

    row32 = lax.broadcasted_iota(jnp.int32, (32, 128), 0)
    lane = lax.broadcasted_iota(jnp.int32, (32, 128), 1)
    group = lane // 32
    eye = jnp.where(lane % 32 == row32, 1.0, 0.0).astype(F32)
    r128 = lax.broadcasted_iota(jnp.int32, (128, 128), 0)
    c128 = lax.broadcasted_iota(jnp.int32, (128, 128), 1)
    blocks = [(p, d) for p in range(PANELS) for d in range(4)]
    comp, ts, pvs, vs = [], [], [], []
    for p, d in blocks:
        u = lv[BLOCK[(p, p)], 128 * d:128 * d + 128, 128 * d:128 * d + 128]
        c = jnp.zeros((32, 128), F32)
        for b in range(4):
            c = jnp.where(group == b, u[32 * b:32 * b + 32, :], c)
        comp.append(c)
        ts.append(eye)
        pvs.append(1.0 / jnp.broadcast_to(piv[p:p + 1, 128 * d:128 * d + 128], (8, 128)))
        vs.append(jnp.zeros((32, 128), F32))
    for j in range(31, -1, -1):
        idx = group * 32 + j
        for n in range(len(blocks)):
            pj = jnp.take_along_axis(pvs[n], idx[:8], axis=1)
            vj = jnp.broadcast_to(ts[n][j:j + 1, :] * pj[0:1, :], (32, 128))
            vs[n] = jnp.where(row32 == j, vj, vs[n])
            if j:
                uj = jnp.take_along_axis(comp[n], idx, axis=1)
                ts[n] = jnp.where(row32 < j, ts[n] - uj * vj, ts[n])
    full = [jnp.concatenate([jnp.where(group == b, v, 0.0) for b in range(4)], 0) for v in vs]
    for s in (32, 64):
        off = (r128 // (2 * s) == c128 // (2 * s)) & (r128 // s % 2 == 0) & (c128 // s % 2 == 1)
        ms = []
        for n, (p, d) in enumerate(blocks):
            u = lv[BLOCK[(p, p)], 128 * d:128 * d + 128, 128 * d:128 * d + 128]
            ms.append(dot3(split(jnp.where(off, u, 0.0)), split(full[n]), NN))
        full = [v - dot3(split(v), split(m), NN) for v, m in zip(full, ms)]
    for n, (p, d) in enumerate(blocks):
        hi, lo = split(full[n])
        vh[p, d] = hi
        vl[p, d] = lo
    outs[2].start()
    outs[3].start()
    for c in outs:
        c.wait()


def prep(tab, pivots, own, other):
    hbm = pl.BlockSpec(memory_space=pl.ANY)
    vmem = pl.BlockSpec(memory_space=pltpu.VMEM)
    big = jax.ShapeDtypeStruct((6, PANEL, PANEL), BF16)
    small = jax.ShapeDtypeStruct((PANELS, 4, 128, 128), BF16)
    return pl.pallas_call(
        prep_body,
        out_shape=[big, big, small, small],
        in_specs=[pl.BlockSpec(memory_space=pltpu.SMEM), vmem, hbm, hbm],
        out_specs=[pl.BlockSpec(memory_space=pltpu.HBM)] * 4,
        scratch_shapes=[
            pltpu.VMEM((6, PANEL, PANEL), F32),
            pltpu.VMEM((6, PANEL, PANEL), BF16),
            pltpu.VMEM((6, PANEL, PANEL), BF16),
            pltpu.VMEM((PANELS, 4, 128, 128), BF16),
            pltpu.VMEM((PANELS, 4, 128, 128), BF16),
            pltpu.SemaphoreType.DMA((6,)),
        ],
        compiler_params=pltpu.CompilerParams(vmem_limit_bytes=28 << 20),
        cost_estimate=pl.CostEstimate(flops=4 << 30, bytes_accessed=14 << 20, transcendentals=0),
        name="prep",
    )(tab, pivots, own, other)


def solve_body(tab, lh_h, ll_h, vh_h, vl_h, rhs, swp, r1, r2, r3, r4, out,
               lh, ll, vh, vl, rv, xh, xl, sem_l, sem_v, sem_r):
    core = tab[0]
    cands = [rhs.at[0, :, pl.ds(pl.multiple_of(core * HALF, HALF), HALF)], swp, r1, r2, r3, r4]
    vcopies = [pltpu.make_async_copy(vh_h, vh, sem_v), pltpu.make_async_copy(vl_h, vl, sem_v)]
    lcopies = {}
    for q in range(PANELS):
        for p in range(q + 1):
            n = BLOCK[(p, q)]
            lcopies[(p, q)] = [pltpu.make_async_copy(lh_h.at[n], lh.at[n], sem_l.at[n]),
                               pltpu.make_async_copy(ll_h.at[n], ll.at[n], sem_l.at[n])]
    for q in range(PANELS):
        for k, cand in enumerate(cands):
            @pl.when(tab[1 + q] == k)
            def _():
                pltpu.make_async_copy(cand.at[pl.ds(0, PANEL)], rv.at[q], sem_r.at[q]).start()
        if q == 0:
            for c in vcopies:
                c.start()
        for p in range(q + 1):
            for c in lcopies[(p, q)]:
                c.start()
    for c in vcopies:
        c.wait()
    for q in range(PANELS):
        pltpu.make_async_copy(r1.at[pl.ds(0, PANEL)], rv.at[q], sem_r.at[q]).wait()
        for p in range(q + 1):
            for c in lcopies[(p, q)]:
                c.wait()
        diag = BLOCK[(q, q)]
        for h in range(2):
            cols = slice(256 * h, 256 * h + 256)
            acc = rv[q, :, cols]
            for p in range(q):
                n = BLOCK[(p, q)]
                acc = acc - dot3((lh[n], ll[n]), (xh[p, :, cols], xl[p, :, cols]), TN)
            rv[q, :, cols] = acc
        for i in range(4):
            rows = slice(128 * i, 128 * i + 128)
            for h in range(2):
                cols = slice(256 * h, 256 * h + 256)
                t = rv[q, rows, cols]
                if i:
                    t = t - dot3((lh[diag, 0:128 * i, rows], ll[diag, 0:128 * i, rows]),
                                 (xh[q, 0:128 * i, cols], xl[q, 0:128 * i, cols]), TN)
                x = dot3((vh[q, i], vl[q, i]), split(t), TN)
                hi, lo = split(x)
                xh[q, rows, cols] = hi
                xl[q, rows, cols] = lo
                out[q, rows, cols] = x


def solve(tab, factors, rhs, swp, recvs):
    hbm = pl.BlockSpec(memory_space=pltpu.HBM)
    vmem = pl.BlockSpec(memory_space=pltpu.VMEM)
    return pl.pallas_call(
        solve_body,
        out_shape=jax.ShapeDtypeStruct((PANELS, PANEL, HALF), F32),
        in_specs=[pl.BlockSpec(memory_space=pltpu.SMEM)] + [hbm] * 10,
        out_specs=vmem,
        scratch_shapes=[
            pltpu.VMEM((6, PANEL, PANEL), BF16),
            pltpu.VMEM((6, PANEL, PANEL), BF16),
            pltpu.VMEM((PANELS, 4, 128, 128), BF16),
            pltpu.VMEM((PANELS, 4, 128, 128), BF16),
            pltpu.VMEM((PANELS, PANEL, HALF), F32),
            pltpu.VMEM((PANELS, PANEL, HALF), BF16),
            pltpu.VMEM((PANELS, PANEL, HALF), BF16),
            pltpu.SemaphoreType.DMA((6,)),
            pltpu.SemaphoreType.DMA,
            pltpu.SemaphoreType.DMA((PANELS,)),
        ],
        compiler_params=pltpu.CompilerParams(vmem_limit_bytes=28 << 20),
        cost_estimate=pl.CostEstimate(flops=8 << 30, bytes_accessed=14 << 20, transcendentals=0),
        name="solve",
    )(tab, *factors, rhs, swp, *recvs)


def update_body(tab_ref, xa_hbm, xb_hbm, *refs):
    bufs = (refs[:4], refs[4:8])
    work_ref, out_ref, solved, xv, xh, xl, fv, sem_x, sem_f = refs[8:]
    step = pl.program_id(0)
    b = step // 2
    core = tab_ref[0]
    row = tab_ref[1]
    xc = [[pltpu.make_async_copy(src.at[p], xv.at[p, :, pl.ds(pl.multiple_of(h * HALF, HALF), HALF)], sem_x.at[p])
           for src, h in ((xa_hbm, core), (xb_hbm, 1 - core))] for p in range(PANELS)]
    out_copy = pltpu.make_async_copy(xv, solved, sem_x.at[PANELS])

    def fcopies(color, inner, slot):
        for q in range(4):
            for i in range(4):
                s = pl.ds(pl.multiple_of(tab_ref[2 + color * 16 + q * 4 + i] * SHARE, SHARE), SHARE)
                yield pltpu.make_async_copy(bufs[color][q].at[i, inner], fv.at[slot, :, s, :], sem_f.at[slot])

    def start(which, slot):
        for color in range(2):
            for inner in range(2):
                @pl.when(which == color * 2 + inner)
                def _():
                    for c in fcopies(color, inner, slot):
                        c.start()

    slot = lax.rem(b, 2)

    def panel(p, cols):
        keep = jnp.logical_or(b > 0, row > p)
        return jnp.where(keep, fv[slot, p, :, cols], 0.0)

    @pl.when(step == 0)
    def _():
        start(0, 0)
        for p in range(PANELS):
            for c in xc[p]:
                c.start()
        start(1, 1)
        for c in fcopies(0, 0, 0):
            c.wait()
        acc = work_ref[0]
        for p in range(PANELS):
            for c in xc[p]:
                c.wait()
            rows = slice(p * PANEL, p * PANEL + PANEL)
            hi, lo = split(xv[p])
            xh[rows, :] = hi
            xl[rows, :] = lo
            acc = acc - dot3(split(panel(p, slice(0, 256))), (hi, lo), TN)
        out_copy.start()
        out_ref[0] = acc

    @pl.when((lax.rem(step, 2) == 0) & (step > 0))
    def _():
        for c in fcopies(0, 0, slot):
            c.wait()

    @pl.when(step > 0)
    def _():
        cols = pl.ds(pl.multiple_of(lax.rem(step, 2) * 256, 256), 256)
        f = jnp.concatenate([panel(p, cols) for p in range(PANELS)], 0)
        out_ref[0] = work_ref[0] - dot3(split(f), (xh[...], xl[...]), TN)

    @pl.when((lax.rem(step, 2) == 1) & (b + 2 < 4))
    def _():
        start(b + 2, slot)

    @pl.when(step == 7)
    def _():
        out_copy.wait()


def update(tab, xa, xb, bufs_a, bufs_b, work):
    wspec = pl.BlockSpec((1, 256, NCOL), lambda s, t: (s // 2, s % 2, 0))
    hbm = pl.BlockSpec(memory_space=pltpu.HBM)
    return pl.pallas_call(
        update_body,
        out_shape=[jax.ShapeDtypeStruct(work.shape, F32), jax.ShapeDtypeStruct((PANELS, PANEL, NCOL), F32)],
        grid_spec=pltpu.PrefetchScalarGridSpec(
            num_scalar_prefetch=1, grid=(8,),
            in_specs=[hbm] * 10 + [wspec],
            out_specs=[wspec, pl.BlockSpec(memory_space=pltpu.HBM)],
            scratch_shapes=[
                pltpu.VMEM((PANELS, PANEL, NCOL), F32),
                pltpu.VMEM((PANELS * PANEL, NCOL), BF16),
                pltpu.VMEM((PANELS * PANEL, NCOL), BF16),
                pltpu.VMEM((2, PANELS, PANEL, PANEL), F32),
                pltpu.SemaphoreType.DMA((PANELS + 1,)),
                pltpu.SemaphoreType.DMA((2,)),
            ],
        ),
        compiler_params=pltpu.CompilerParams(vmem_limit_bytes=54 << 20),
        cost_estimate=pl.CostEstimate(flops=20 << 30, bytes_accessed=42 << 20, transcendentals=0),
        name="update",
    )(tab, xa, xb, *bufs_a, *bufs_b, work)


def table(core, make):
    a = jnp.array(make(0), jnp.int32)
    b = jnp.array(make(1), jnp.int32)
    return jnp.where(core == 0, a, b)


def wave_masks(core, color):
    m = STEPS[(core, color)]
    low = [(m[0] if i & 1 else 0) ^ (m[1] if i & 2 else 0) for i in range(4)]
    return low, [v ^ m[2] for v in low], [v ^ m[3] for v in low], [v ^ m[2] ^ m[3] for v in low]


def panels(factor, pivots, rhs):
    row = lax.axis_index("row")
    col = lax.axis_index("col")
    core, z = row % 2, row // 2
    x, y = col // 4, col % 4
    first = core == 0

    swl = swap_cores(factor[0, 2])
    pay = factor[0, 0:2]
    pay = jnp.where((core == 1) & (z == 1), jnp.broadcast_to(swl[None], pay.shape), pay)
    pay, later_factor, slab = lax.optimization_barrier((pay, factor, rhs))
    got = z_xor(pay, 1)
    low = jnp.where(z == 0, pay, got)
    high = jnp.where(z == 0, got, pay)
    share = jnp.where(first, jnp.stack([low[0], high[0], high[1]]), jnp.stack([low[0], low[1], high[0]]))

    theirs = lax.dynamic_slice(slab, (0, 0, (1 - core) * HALF), (1, PANEL, HALF))[0]
    mine = lax.dynamic_slice(slab, (0, 0, core * HALF), (1, PANEL, HALF))[0]
    swp = swap_cores(theirs)
    half_a, half_b = later_factor[0:2][None], later_factor[2:4][None]
    ra1 = xor_wave(half_a, 0, 0)
    rb1 = xor_wave(half_b, 1, 0)
    share = jnp.where(z < 2, share, z_xor(share, 3))

    r1 = z_ring(jnp.where(first, mine, swp))
    r2 = z_ring(jnp.where(z == 0, jnp.where(first, swp, mine), r1))
    r3 = z_ring(jnp.where((z == 0) & (core == 1), r1, r2))
    r4 = z_ring(r3)

    def place(which):
        cols = []
        for k in range(4):
            for j in range(4):
                if which == 0:
                    cols.append((x + OFFSETS[j]) % 4 * 4 + (y + OFFSETS[k]) % 4)
                else:
                    cols.append((x + OFFSETS[k]) % 4 * 4 + (y + OFFSETS[j]) % 4)
        return jnp.stack(cols)

    rtab = jnp.array([[[0, 1, 4], [2, 3, 0], [3, 4, 2], [4, 5, 3]],
                      [[1, 0, 2], [4, 5, 1], [3, 4, 5], [2, 3, 4]]], jnp.int32)
    stab = jnp.concatenate([core[None], rtab[core, z], jnp.where(first, place(0), place(1))]).astype(jnp.int32)

    one = share[None]
    (ph1,) = join([one] + [shift(one, 0, s) for s in (1, 3, 2)])
    lown = pack(stab, [ph1] + [shift(ph1, 1, s) for s in (1, 3, 2)])
    loth = swap_cores(lown)

    fa, fb = join([half_a, ra1], [half_b, rb1])
    ra2, rb2 = xor_wave(fa, 0, 1), xor_wave(fb, 1, 1)
    fa, fb = join([fa, ra2], [fb, rb2])
    ga, gb = xor_wave(fa, 0, 2), xor_wave(fb, 1, 2)
    ha, hb = xor_wave(fa, 0, 3), xor_wave(fb, 1, 3)
    ka, kb = xor_wave(ga, 0, 3), xor_wave(gb, 1, 3)

    factors = prep(stab, pivots, lown, loth)
    xa = solve(stab, factors, rhs, swp, (r1, r2, r3, r4))
    xb = swap_cores(xa)

    def make(c):
        return [v for color in range(2) for part in wave_masks(c, color) for v in part]

    utab = jnp.concatenate([core[None], row[None], table(core, make) ^ col]).astype(jnp.int32)
    work, solved = update(utab, xa, xb, (fa, ga, ha, ka), (fb, gb, hb, kb), rhs)
    return solved, work


def solution(mesh):
    return jax.shard_map(
        panels,
        mesh=mesh,
        in_specs=(P(None, None, "col", "row"), P(), P(None, "row", "col")),
        out_specs=(P(None, None, "col"), P(None, "row", "col")),
        check_vma=False,
    )
```
